32 devices in a mesh: row: 8 (over y, x, core), col: 4 (over z).
Axes of the slice: x: 2, y: 2, z: 4, core: 2. Of those that a mesh axis runs over, the one named last changes fastest.
Arguments:
- hessian: float32 [8, 2048, 16, 1024], P(None, 'row', None, 'col'), as said below
Outputs:
- factored: float32 [8, 2048, 16, 1024], P(None, 'row', None, 'col')
Inputs may be any that keep to these rules, and one draw needn't show every extreme that they name: hessian, read as the 16384 x 16384 matrix H0, is symmetric and positive definite.
All inputs are finite; a program needn't handle non-finite values.
Results may differ from the reference program's by a relative error of at most 0.0003.
Values sent between devices are 32-bit elements; how exact they have to be, the bound alone decides.
No kernel may reach another device: no remote copies, remote signals or barrier semaphores. Data moves between devices by JAX's collectives and lax.ppermute only.
A program may use at most 192 MiB of HBM per device.

```python
import jax
import jax.numpy as jnp
from jax import lax

N = 16384
BLOCK = 256
SAMPLES = 1024
RCYC = 8
CCYC = 16


def draw_hessian(key, part):
    base = jax.random.fold_in(key, 7)
    key_scale, key_data, key_damp = jax.random.split(base, 3)
    scales = jnp.exp(jax.random.uniform(key_scale, (N, 1), jnp.float32, jnp.log(0.3), jnp.log(3.0)))
    samples = jax.random.normal(key_data, (N, SAMPLES), jnp.float32) * scales
    gram = jnp.dot(samples, samples.T, precision=lax.Precision.HIGHEST) / SAMPLES
    damping = jax.random.uniform(key_damp, (N,), jnp.float32, 0.05, 0.5) * scales[:, 0] * scales[:, 0]
    places = jnp.arange(N, dtype=jnp.int32)
    gram = gram.at[places, places].add(damping)
    return gram.reshape(RCYC, N // RCYC, CCYC, N // CCYC)


def setup_inputs(seed: int = 0) -> dict:
    seeds = jax.random.split(jax.random.key(seed), 2)
    return {
        "hessian": draw_hessian(jax.random.fold_in(seeds[1], 71), 0),
    }


def reference(hessian):
    matrix = hessian.reshape(N, N)
    identity = jnp.eye(BLOCK, dtype=matrix.dtype)
    positions = jnp.arange(N, dtype=jnp.int32)
    offsets = jnp.arange(BLOCK, dtype=jnp.int32)
    panels = []
    for panel_index in range(2):
        start = panel_index * BLOCK
        diagonal = matrix[start:start + BLOCK, start:start + BLOCK]
        lower_factor = jnp.linalg.cholesky(diagonal)
        inverse = lax.linalg.triangular_solve(lower_factor, identity, left_side=True, lower=True)
        own_panel = jnp.dot(matrix[:, start:start + BLOCK], inverse.T, precision=lax.Precision.HIGHEST)
        keep_mask = positions[:, None] >= start + offsets[None, :]
        own_panel = jnp.where(keep_mask, own_panel, jnp.zeros_like(own_panel))
        matrix = matrix - jnp.dot(own_panel, own_panel.T, precision=lax.Precision.HIGHEST)
        panels.append(own_panel)
    result = matrix.at[:2 * BLOCK, 2 * BLOCK:].set(0.0)
    result = result.at[:, :2 * BLOCK].set(jnp.concatenate(panels, axis=1))
    return result.reshape(RCYC, N // RCYC, CCYC, N // CCYC)
```

```python
import functools

import jax
import jax.numpy as jnp
from jax import lax
from jax.experimental import pallas as pl
from jax.experimental.pallas import tpu as pltpu
from jax.sharding import PartitionSpec as P


S=8; T=128
HI=lax.Precision.HIGHEST
F32=jnp.float32; BF=jnp.bfloat16
VM=pl.BlockSpec(memory_space=pltpu.VMEM)
CP=pltpu.CompilerParams(vmem_limit_bytes=60000*1024)
def split(x):
    hi=x.astype(BF)
    return hi,(x-hi.astype(F32)).astype(BF)
def extract(view,rows,n):
    def k(a_ref,b_ref,o_ref):
        for ch,r in enumerate((a_ref,b_ref)):
            o_ref[:,ch*T:(ch+1)*T]=r.reshape(n*S,T)[pl.ds(0,n,stride=S),:]
    return pl.pallas_call(k,grid=(rows//n,),out_shape=jax.ShapeDtypeStruct((rows,2*T),F32),
        in_specs=[pl.BlockSpec((n,None,S,T),lambda i,c=ch:(i,c,0,0)) for ch in range(2)],
        out_specs=pl.BlockSpec((n,2*T),lambda i:(i,0)),name="extract",compiler_params=CP)(view,view)
def project(me,lead,v):
    m,tiles=lead[0].shape[:2]; w=2*m
    def k(me_ref,*refs):
        v_ref,h_ref,l_ref=refs[4:]
        even=me_ref[0]%2==0
        flat=[r.reshape(m*S,T) for r in refs[:4]]
        def read(p):
            x=[jnp.concatenate([f[pl.ds(2*p+u,m,stride=S),:] for u in range(2)],1) for f in flat]
            mine=jnp.concatenate(x[:2],0); theirs=jnp.concatenate(x[2:],0)
            return jnp.where(even,mine,theirs),jnp.where(even,theirs,mine)
        for p in range(S//2):
            a,b=read(p)
            q0=jnp.dot(v_ref[0:w,0:w],a,precision=HI,preferred_element_type=F32)
            q1=jnp.dot(v_ref[w:2*w,0:w],a,precision=HI,preferred_element_type=F32)+jnp.dot(v_ref[w:2*w,w:2*w],b,precision=HI,preferred_element_type=F32)
            cs=slice(2*p*T,2*p*T+2*T)
            h_ref[0:w,cs],l_ref[0:w,cs]=split(q0)
            h_ref[w:2*w,cs],l_ref[w:2*w,cs]=split(q1)
    o=jax.ShapeDtypeStruct((2*w,tiles*S*T),BF)
    gs=pltpu.PrefetchScalarGridSpec(num_scalar_prefetch=1,grid=(tiles,),
        in_specs=[pl.BlockSpec((m,None,S,T),lambda j,me:(0,j,0,0))]*4+[VM],
        out_specs=[pl.BlockSpec((2*w,S*T),lambda j,me:(0,j))]*2)
    return pl.pallas_call(k,grid_spec=gs,out_shape=(o,o),name="project",compiler_params=CP)(me,*lead,v)
def update(where_am_i,view,a0,a1,v,qh,ql,n):
    rows,tiles=view.shape[:2]; w=a0.shape[1]; d=2*w
    def k(me_ref,h_ref,a_ref,b_ref,v_ref,qh_ref,ql_ref,o_ref,ph,pl_,pf):
        i=pl.program_id(0); j=pl.program_id(1)
        row=me_ref[0]; col=me_ref[1]
        nt=(((1,),(1,)),((),()))
        @pl.when(j==0)
        def _():
            p0=lax.dot_general(a_ref[...],v_ref[0:w,0:w],nt,precision=HI,preferred_element_type=F32)
            p1=lax.dot_general(a_ref[...],v_ref[w:d,0:w],nt,precision=HI,preferred_element_type=F32)+lax.dot_general(b_ref[...],v_ref[w:d,w:d],nt,precision=HI,preferred_element_type=F32)
            for s,p in enumerate((p0,p1)):
                ph[:,s*w:(s+1)*w],pl_[:,s*w:(s+1)*w]=split(p)
            pf[...]=jnp.where(col==0,p0,p1)
        hf=h_ref.reshape(n*S,T); of=o_ref.reshape(n*S,T)
        for p in range(S//2):
            cs=pl.ds(pl.multiple_of(j*(S*T)+2*p*T,2*T),2*T)
            x=jnp.dot(ph[...],qh_ref[:,cs],preferred_element_type=F32)
            x=x+jnp.dot(ph[...],ql_ref[:,cs],preferred_element_type=F32)
            x=x+jnp.dot(pl_[...],qh_ref[:,cs],preferred_element_type=F32)
            for u in range(2):
                rs=pl.ds(2*p+u,n,stride=S)
                of[rs,:]=hf[rs,:]-x[:,u*T:(u+1)*T]
        first=i==0
        @pl.when(first&(row<2))
        def _():
            o_ref[0:w]=jnp.zeros((w,S,T),F32)
        nch=w//T
        @pl.when((col<2)&(j<nch))
        def _():
            half=pf[:,0:T]
            for ch in range(1,nch): half=jnp.where(j==ch,pf[:,ch*T:(ch+1)*T],half)
            r=lax.broadcasted_iota(jnp.int32,(n,T),0); c=lax.broadcasted_iota(jnp.int32,(n,T),1)+j*T
            top=first&(row<2)
            keep=(r+row*w>=c+col*w)|(r>=w)|jnp.logical_not(top)
            of[pl.ds(0,n,stride=S),:]=jnp.where(keep,half,0.0)
    gs=pltpu.PrefetchScalarGridSpec(num_scalar_prefetch=1,grid=(rows//n,tiles),
        in_specs=[pl.BlockSpec((n,None,S,T),lambda i,j,m:(i,j,0,0)),pl.BlockSpec((n,w),lambda i,j,m:(i,0)),pl.BlockSpec((n,w),lambda i,j,m:(i,0)),VM,VM,VM],
        out_specs=pl.BlockSpec((n,None,S,T),lambda i,j,m:(i,j,0,0)),
        scratch_shapes=[pltpu.VMEM((n,d),BF),pltpu.VMEM((n,d),BF),pltpu.VMEM((n,w),F32)])
    return pl.pallas_call(k,grid_spec=gs,out_shape=jax.ShapeDtypeStruct(view.shape,F32),name="update",compiler_params=CP)(where_am_i,view,a0,a1,v,qh,ql)

def spread(v): return jnp.broadcast_to(v,(S,T))
def factor_tile(g):
    lane=lax.broadcasted_iota(jnp.int32,(S,T),1); sub=lax.broadcasted_iota(jnp.int32,(S,T),0)
    n=len(g)
    for t in range(n):
        x=g[t]; lo=S*t
        c=[spread(x[:,lo+i:lo+i+1]) for i in range(S)]
        for j in range(S):
            p=spread(c[j][j:j+1,:])
            r=lax.rsqrt(p)
            inv=r*r
            col=jnp.where(sub>j,c[j],0.0)
            here=lane==lo+j
            row=spread(x[j:j+1,:])
            for i in range(j+1,S):
                c[i]=c[i]-(col*spread(c[i][j:j+1,:]))*inv
            grow=jnp.where(here,r,row*r)
            x=jnp.where(sub==j,grow,jnp.where(here,0.0,x)-(col*r)*grow)
        g[t]=x
        if t<n-1:
            xt=x.T
            rows=[spread(x[j:j+1,:]) for j in range(S)]
            panel=(lane>=lo)&(lane<lo+S)
            for b in range(t+1,n):
                acc=jnp.where(panel,0.0,g[b])
                xb=xt[S*b:S*b+S,:]
                for j in range(S):
                    acc=acc-spread(xb[:,j:j+1])*rows[j]
                g[b]=acc
    return g
def fkernel(d00,d01,d11,v_ref,g):
    w=d00.shape[0]; n=2*w; nb=n//T
    g[0:w,0:w]=d00[...]; g[0:w,w:n]=d01[...]; g[w:n,w:n]=d11[...]; g[w:n,0:w]=jnp.zeros((w,w),jnp.float32)
    row=lax.broadcasted_iota(jnp.int32,(T,T),0); lane=lax.broadcasted_iota(jnp.int32,(T,T),1)
    for kb in range(nb):
        b=kb*T
        tiles=factor_tile([g[b+S*i:b+S*i+S,b:b+T] for i in range(T//S)])
        vk=jnp.where(lane<=row,jnp.concatenate(tiles,0),0.0)
        left=[jnp.dot(vk,g[b:b+T,0:b],precision=HI,preferred_element_type=jnp.float32)] if kb else []
        right=[jnp.dot(vk,g[b:b+T,b+T:n],precision=HI,preferred_element_type=jnp.float32)] if kb<nb-1 else []
        r=jnp.concatenate(left+[vk]+right,1)
        v_ref[b:b+T,:]=jnp.concatenate(left+[vk]+[jnp.zeros_like(x) for x in right],1)
        if right:
            g[b+T:n,b:b+T]=jnp.zeros((n-b-T,T),jnp.float32)
            u=lax.dot_general(right[0],r,(((0,),(0,)),((),())),precision=HI,preferred_element_type=jnp.float32)
            g[b+T:n,:]=g[b+T:n,:]-u
def factor(d00,d01,d11):
    n=2*d00.shape[0]
    vm=pl.BlockSpec(memory_space=pltpu.VMEM)
    return pl.pallas_call(fkernel,out_shape=jax.ShapeDtypeStruct((n,n),jnp.float32),in_specs=[vm]*3,out_specs=vm,
       scratch_shapes=[pltpu.VMEM((n,n),jnp.float32)],name="factor",compiler_params=CP)(d00,d01,d11)


def broadcast(x, axis, root):
    mine = lax.axis_index(axis) == root
    return lax.psum(jnp.where(mine, x, jnp.zeros_like(x)), axis)


def invert_factor(diagonal):
    lower_factor = jnp.linalg.cholesky(diagonal)
    identity = jnp.eye(diagonal.shape[0], dtype=diagonal.dtype)
    return lax.linalg.triangular_solve(lower_factor, identity, left_side=True, lower=True)


def outer_update(own_panel, across):
    row_cycles, block_width, depth = own_panel.shape
    column_count = across.shape[0]
    product_flat = jnp.dot(
        own_panel.reshape(row_cycles * block_width, depth),
        across.reshape(column_count * block_width, depth).T,
        precision=lax.Precision.HIGHEST,
    )
    return product_flat.reshape(row_cycles, block_width, column_count, block_width)


def general_on_device(hessian):
    row_count = lax.axis_size("row")
    column_count = lax.axis_size("col")
    row_index = lax.axis_index("row")
    column_index = lax.axis_index("col")
    row_cycles, block_width, column_cycles, _ = hessian.shape
    row_blocks = row_index + row_count * jnp.arange(row_cycles, dtype=jnp.int32)
    col_blocks = column_index + column_count * jnp.arange(column_cycles, dtype=jnp.int32)
    offsets = jnp.arange(block_width, dtype=jnp.int32)
    row_position = row_blocks[:, None] * block_width + offsets[None, :]

    def apply_factor(column, inverse, panel_index):
        own_panel = jnp.dot(
            column.reshape(row_cycles * block_width, block_width),
            inverse.T,
            precision=lax.Precision.HIGHEST,
        )
        own_panel = own_panel.reshape(row_cycles, block_width, block_width)
        keep_mask = row_position[:, :, None] >= panel_index * block_width + offsets[None, None, :]
        return jnp.where(keep_mask, own_panel, jnp.zeros_like(own_panel))

    matrix = hessian
    slabs = []
    for root_col in range(2):
        slabs.append(broadcast(matrix[:, :, 0, :], "col", root_col))
    leading = jnp.stack(slabs, axis=2)
    blocks = []
    for root_row in range(2):
        blocks.append(broadcast(leading[0], "row", root_row))
    upper_rows, lower_rows = blocks
    first_inverse = invert_factor(upper_rows[:, 0, :])
    lower_first = jnp.dot(lower_rows[:, 0, :], first_inverse.T, precision=lax.Precision.HIGHEST)
    second_diag = lower_rows[:, 1, :] - jnp.dot(
        lower_first, lower_first.T, precision=lax.Precision.HIGHEST
    )
    second_inverse = invert_factor(second_diag)
    first_panel = apply_factor(leading[:, :, 0, :], first_inverse, 0)
    first_flat = first_panel.reshape(row_cycles * block_width, block_width)
    second_column = leading[:, :, 1, :] - jnp.dot(
        first_flat, lower_first.T, precision=lax.Precision.HIGHEST
    ).reshape(row_cycles, block_width, block_width)
    second_panel = apply_factor(second_column, second_inverse, 1)
    both_panels = jnp.concatenate([first_panel, second_panel], axis=2)
    depth = both_panels.shape[2]
    pieces = []
    for root_half in range(2):
        pieces.append(broadcast(both_panels, "row", column_index + root_half * column_count))
    across = jnp.stack(pieces, axis=1)
    both_across = across.reshape(column_cycles, block_width, depth)
    matrix = matrix - outer_update(both_panels, both_across)
    row_global = row_blocks[:, None, None, None]
    col_global = col_blocks[None, None, :, None]
    result = jnp.where(row_global < 2, jnp.zeros_like(matrix), matrix)
    result = jnp.where(col_global == 0, first_panel[:, :, None, :], result)
    result = jnp.where(col_global == 1, second_panel[:, :, None, :], result)
    return result


def permute(x, pairs):
    return lax.ppermute(x, ("row", "col"), pairs)


def on_device(hessian):
    row_count = lax.axis_size("row")
    col_count = lax.axis_size("col")
    row = lax.axis_index("row")
    col = lax.axis_index("col")
    row_cycles, width, col_cycles, _ = hessian.shape
    rows = row_cycles * width
    chunks = width // T
    tiles = col_cycles // S * chunks
    core = row % 2
    flat = lambda r, c: r * col_count + c

    view = hessian.reshape(rows, col_cycles // S, S, chunks, T)
    view = view.transpose(0, 1, 3, 2, 4).reshape(rows, tiles, S, T)
    slab = extract(view, rows, width)

    bits = [1 << b for b in range(1, row_count.bit_length() - 1)]

    def spread_rows(x, order):
        seen = 1
        for bit in order:
            pairs = [
                (flat(r, c), flat(r | bit, c))
                for r in range(row_count)
                if r & ~seen == 0
                for c in range(col_count)
            ]
            received = permute(x, pairs)
            x = jnp.where((row & ~seen) == 0, x, received)
            seen |= bit
        return x

    def swap_core(x, from_cores=(0, 1)):
        pairs = [
            (flat(r, c), flat(r ^ 1, c))
            for r in range(row_count)
            if r % 2 in from_cores
            for c in range(col_count)
        ]
        return permute(x, pairs)

    corner = slab[0:width]
    mine = corner
    for k in range(2, col_count, 2):
        pairs = [(flat(r, s), flat(r, s + k)) for r in range(2) for s in range(2)]
        received = permute(corner, pairs)
        mine = jnp.where(col < 2, corner, received) if k == 2 else mine + received
    pairs = [(flat(r, c), flat(r, c ^ 1)) for r in range(2) for c in range(col_count)]
    other = permute(mine, pairs)
    even = jnp.where(col % 2 == 0, mine, other)
    odd = jnp.where(col % 2 == 0, other, mine)
    even = spread_rows(even, bits)
    odd = spread_rows(odd, bits[::-1])
    even_other = swap_core(even, (0,))
    odd_other = swap_core(odd)
    corner_00 = jnp.where(core == 0, even, even_other)
    corner_01 = jnp.where(core == 0, odd, odd_other)
    corner_11 = jnp.where(core == 0, odd_other, odd)
    inverse = factor(corner_00, corner_01, corner_11)

    half = width // 2
    upper = spread_rows(view[0:half], bits)
    lower = spread_rows(view[half:width], bits[::-1])
    lead = (upper, lower, swap_core(upper), swap_core(lower))

    part = rows // 2
    lefts, rights = [], []
    for s in range(2):
        own = slab[s * part:(s + 1) * part]
        swapped = permute(own, [(flat(r, c), flat(r, c ^ 1)) for r in range(row_count) for c in range(2)])
        left = jnp.where(col == 0, own, swapped)
        right = jnp.where(col == 0, swapped, own)
        hop_left, hop_right = swapped, own
        for c in range(1, col_count - 1):
            pairs = [(flat(r, c), flat(r, c + 1)) for r in range(row_count)]
            hop_right = permute(hop_right, pairs)
            hop_left = permute(hop_left, pairs)
            left = jnp.where(col == c + 1, hop_left, left)
            right = jnp.where(col == c + 1, hop_right, right)
        lefts.append(left)
        rights.append(right)
    left = jnp.concatenate(lefts, 0)
    right = jnp.concatenate(rights, 0)

    place = jnp.stack([row, col]).astype(jnp.int32)
    high, low = project(place, lead, inverse)
    result = update(place, view, left, right, inverse, high, low, 2 * width)
    result = result.reshape(rows, col_cycles // S, chunks, S, T).transpose(0, 1, 3, 2, 4)
    return result.reshape(hessian.shape)


def solution(mesh):
    row_count, col_count = mesh.shape["row"], mesh.shape["col"]

    def step(hessian):
        row_cycles, width, col_cycles, _ = hessian.shape
        pairs = row_count & (row_count - 1) == 0 and row_count > 1 and col_count % 2 == 0
        if pairs and width == 2 * T and col_cycles % S == 0 and row_cycles % 2 == 0:
            return on_device(hessian)
        return general_on_device(hessian)

    spec = P(None, "row", None, "col")
    return jax.shard_map(step, mesh=mesh, in_specs=(spec,), out_specs=spec, check_vma=False)
```
